512 devices in a mesh: grp: 16 (over z), mem: 32 (over y, x, core).
Axes of the slice: x: 4, y: 4, z: 16, core: 2. Of those that a mesh axis runs over, the one named last changes fastest.
Arguments:
- bin_sketch: bfloat16 [4096, 1024], P(('grp', 'mem')), may hold values from -6 to 6
- rep_sketch: bfloat16 [131072, 1024], P(('grp', 'mem')), may hold values from -6 to 6
- bin_profile: bfloat16 [4096, 32768], P('grp', 'mem'), may hold values from -6 to 6
- member_profile: bfloat16 [48, 256, 32768], P('grp', None, 'mem'), may hold values from -6 to 6
- bin_routes: int32 [4096, 2], P('grp'), may hold values from 0 to 47, all different within a row; in each aligned block of 256 rows (0 to 255, 256 to 511, ...) at most 16 rows name the same one
- owner_slot: int32 [48], replicated, may hold values from 0 to 47, each once
- cluster_sizes: int32 [48], replicated, may hold values from 128 to 256, as said below
Outputs:
- coarse_scores: bfloat16 [4096, 131072], P(None, ('grp', 'mem'))
- fine_scores: float32 [4096, 2, 256], P('grp', None, 'mem')
The draws below stay inside these ranges and needn't reach their ends.
Inputs may be any that keep to these rules, and one draw needn't show every extreme that they name: `bin_routes`: within the bins of one index of grp (256 consecutive bins), no cluster is named by more than 16 routes, a bound that some block reaches; the two clusters of a bin differ. `owner_slot`: A permutation. `cluster_sizes`: each a multiple of 128.
All inputs are finite; a program needn't handle non-finite values.
Results may differ from the reference program's by a relative error of at most 0.001.
Values may be sent and summed in bfloat16 or wider, within the bound.
A program may use at most 128 MiB of HBM per device.

```python
import math
import jax
import jax.numpy as jnp
import numpy as np
from jax import lax

W = 1024
FW = 32768
MEMBERS = 256
BIN_DEV = 8
BINS = 4096
REPS = 131072
CLUSTERS = 48
MOST = 16
BLOCK = 128
N_GRP = 16
N_MEM = 32


def draw_cluster_sizes(key, part):
    first_key = jax.random.fold_in(key, 11)
    second_key = jax.random.fold_in(key, 12)
    third_key = jax.random.fold_in(key, 13)
    blocks_each = jax.random.randint(first_key, (CLUSTERS,), 1, 3)
    small_one = jax.random.randint(second_key, (), 0, CLUSTERS)
    large_one = (small_one + 1 + jax.random.randint(third_key, (), 0, CLUSTERS - 1)) % CLUSTERS
    position = jnp.arange(CLUSTERS)
    blocks_each = jnp.where(position == small_one, 1, blocks_each)
    blocks_each = jnp.where(position == large_one, 2, blocks_each)
    return (blocks_each * BLOCK).astype(jnp.int32)


def block_scale(own_key, dims, split, low, largest):
    def one(axis_at, blocks):
        steps = jax.random.uniform(jax.random.fold_in(jax.random.fold_in(own_key, 6), axis_at), (blocks,), jnp.float32, low / len(split), largest / len(split))
        return jnp.repeat(jnp.exp(steps), dims[axis_at] // blocks).reshape((-1,) + (1,) * (len(dims) - axis_at - 1))

    gain = one(*split[0])
    for cut in split[1:]:
        gain = gain * one(*cut)
    return gain


def routed_block(key, own, number, rows, count, top, most, skew):
    order = jax.random.permutation(key, count)
    packed, usual = portions_of(count, rows * top, most, skew, True), portions_of(count, rows * top, most, skew, False)
    places = jnp.arange(count)

    def named(lengths, rotation):
        used = int((lengths > 0).sum())
        fixed = max(1, used // 4)
        moved = fixed + (places - fixed + rotation * (used - fixed)) % max(1, count - fixed)
        return jnp.zeros((count,), jnp.int32).at[order[jnp.where(places < fixed, places, moved)]].set(jnp.asarray(lengths, jnp.int32))

    lengths = jnp.where(number % 4 == 0, named(packed, number // 4), named(usual, number - number // 4 - 1))
    mixed = jax.random.permutation(jax.random.fold_in(own, 3), count)
    giver, sink = mixed[0:count // 2 * 2:2], mixed[1:count // 2 * 2:2]
    slack = jnp.minimum(lengths[giver] - 1, most - lengths[sink]) // 2
    slack = jnp.where((giver == order[0]) | (sink == order[0]) | (lengths[sink] == 0), 0, jnp.maximum(slack, 0))
    moved = jax.random.randint(jax.random.fold_in(own, 4), (count // 2,), 0, 1 << 20) % (slack + 1)
    lengths = lengths.at[giver].add(-moved).at[sink].add(moved)
    members = jnp.searchsorted(jnp.cumsum(lengths), jnp.arange(rows * top), side="right").astype(jnp.int32)
    listing = members.reshape(top, rows).T
    listing = listing[jax.random.permutation(jax.random.fold_in(own, 1), rows)]
    rotation = jax.random.randint(jax.random.fold_in(own, 2), (rows, 1), 0, top)
    return jnp.take_along_axis(listing, (jnp.arange(top)[None, :] + rotation) % top, axis=1)


def portions_of(number_of, total, limit, slope, full):
    loads = [(1 << 20) // math.isqrt(grade ** slope) + 1 for grade in range(1, number_of + 1)]
    largest = limit if full else min(limit, max(-(-total // number_of), total * loads[0] // sum(loads)))
    least = 1 if total - largest >= number_of - 1 else 0
    given, surplus = [largest] + [least] * (number_of - 1), total - largest - least * (number_of - 1)
    while surplus > 0:
        free = [i for i in range(1, number_of) if given[i] < largest] or [i for i in range(1, number_of) if given[i] < limit]
        whole, budget = sum([loads[i] for i in free]), surplus
        for i in free:
            more = min(limit - given[i], max(1, budget * loads[i] // whole), surplus)
            given[i] = given[i] + more
            surplus = surplus - more
    return np.array(given)


def scatter_about(rng, dims, scale, bound, split=(), kind=jnp.bfloat16):
    entries = scale * jax.random.normal(rng, dims, jnp.float32)
    if split:
        entries = entries * block_scale(rng, dims, split, -0.22, 0.18)
    return jnp.clip(entries, -bound, bound).astype(kind)


def setup_inputs(seed: int = 0) -> dict:
    arg_keys = jax.random.split(jax.random.key(seed), 8)
    bin_sketch = scatter_about(arg_keys[0], (BINS, W), 1.0, 6.0, ((0, 512),))
    rep_sketch = scatter_about(arg_keys[1], (REPS, W), 1.0, 6.0, ((0, 512),))
    bin_profile = scatter_about(arg_keys[2], (BINS, FW), 1.0, 6.0, ((0, 16), (1, 32)))
    member_profile = scatter_about(arg_keys[3], (CLUSTERS, MEMBERS, FW), 1.0, 6.0, ((0, 16), (2, 32)))
    bin_routes_keys = jax.random.split(jax.random.fold_in(arg_keys[4], 1), BINS // (BIN_DEV * N_MEM))
    bin_routes_turns = jax.random.permutation(jax.random.fold_in(arg_keys[4], 3), BINS // (BIN_DEV * N_MEM))
    bin_routes = jax.vmap(lambda own, number: routed_block(jax.random.fold_in(arg_keys[4], 2), own, number, BIN_DEV * N_MEM, CLUSTERS, 2, MOST, 2))(bin_routes_keys, bin_routes_turns).reshape((BINS, 2))
    owner_slot = jax.random.permutation(arg_keys[5], CLUSTERS).astype(jnp.int32)
    cluster_sizes = draw_cluster_sizes(jax.random.fold_in(arg_keys[7], 71), 0)
    return {"bin_sketch": bin_sketch, "rep_sketch": rep_sketch, "bin_profile": bin_profile, "member_profile": member_profile, "bin_routes": bin_routes, "owner_slot": owner_slot, "cluster_sizes": cluster_sizes}


def reference(bin_sketch, rep_sketch, bin_profile, member_profile, bin_routes, owner_slot, cluster_sizes):
    coarse_scale = W ** -0.5

    def coarse_block(rows_block):
        product = lax.dot_general(rows_block, rep_sketch, (((1,), (1,)), ((), ())), preferred_element_type=jnp.float32)
        return (product * coarse_scale).astype(jnp.bfloat16)

    block_count = max(BINS // 256, 1)
    blocks = bin_sketch.reshape(block_count, BINS // block_count, W)
    coarse_scores = lax.map(coarse_block, blocks).reshape(BINS, REPS)

    route_flat = bin_routes.reshape(-1)
    route_slot = owner_slot[route_flat]
    capacity = N_GRP * MOST

    def per_cluster(slot_now):
        route_hit = route_slot == slot_now
        picked = jnp.argsort(jnp.where(route_hit, 0, 1).astype(jnp.int32), stable=True)[:capacity].astype(jnp.int32)
        profiles = bin_profile[picked // 2]
        product = lax.dot_general(profiles, member_profile[slot_now], (((1,), (1,)), ((), ())), preferred_element_type=jnp.float32)
        return picked, jnp.where(route_hit[picked][:, None], product, 0.0)

    picked_all, product_all = lax.map(per_cluster, jnp.arange(CLUSTERS, dtype=jnp.int32))
    raw_scores = jnp.zeros((2 * BINS, MEMBERS), jnp.float32).at[picked_all.reshape(-1)].add(product_all.reshape(-1, MEMBERS))
    member_index = jnp.arange(MEMBERS, dtype=jnp.int32)
    member_live = member_index[None, :] < cluster_sizes[route_flat][:, None]
    fine_scores = jnp.where(member_live, raw_scores * (FW ** -0.5), 0.0).reshape(BINS, 2, MEMBERS)
    return coarse_scores, fine_scores
```

```python
import functools

import jax
import jax.numpy as jnp
from jax import lax
from jax.experimental import pallas as pl
from jax.experimental.pallas import tpu as pltpu
from jax.sharding import PartitionSpec as P

MOST = 16
RAW = 3
CHUNKS = 8
QUEUE = 3
BF = jnp.bfloat16
F32 = jnp.float32
I32 = jnp.int32


def compact_list(half, raw):
    return [(h, d) for h in range(raw + 1, half + 1) for d in range(half, h - 1, -1)]


def screen(cfg, bs_ref, rep_hbm, bp_ref, mp_hbm, v_ref, out_ref, fine_ref, *scratch):
    n, m_all, edge, raw_hops = cfg["n"], cfg["m"], cfg["edge"], cfg["raw"]
    (ring, vbuf, cbuf, dbuf, ext, gat, rep, mp, stage, part, red, sums, ret,
     zs, zr, xs, xr, rs, rr, ts, tr, ls, os_) = scratch
    half = n // 2
    messages = compact_list(half, raw_hops)
    grp = lax.axis_index("grp")
    mem = lax.axis_index("mem")
    core = lax.rem(mem, 2)
    sigma = 1 - 2 * core
    chip = mem // 2
    y, x = chip // edge, lax.rem(chip, edge)
    alpha = jnp.where(core == 0, x, y)
    beta = jnp.where(core == 0, y, x)
    bins = bp_ref.shape[0]
    width = bp_ref.shape[1]
    rows = bins // CHUNKS
    slots = mp.shape[0]
    block = slots * MOST

    def group_at(sign, distance):
        return lax.rem(grp + sigma * (sign * distance) + n, n)

    def z_device(sign):
        return {"grp": group_at(sign, 1), "mem": mem}

    def member_at(a, b):
        yy = jnp.where(core == 0, b, a)
        xx = jnp.where(core == 0, a, b)
        return (yy * edge + xx) * 2 + core

    def a_device(i):
        return {"grp": grp, "mem": member_at(lax.rem(alpha + i, edge), beta)}

    def b_device(i):
        return {"grp": grp, "mem": member_at(alpha, lax.rem(beta + i, edge))}

    partner = {"grp": grp, "mem": mem + sigma}

    greeted = [z_device(1), z_device(-1), partner]
    greeted += [a_device(i) for i in range(1, edge)] + [b_device(i) for i in range(1, edge)]
    barrier = pltpu.get_barrier_semaphore()
    for device in greeted:
        pl.semaphore_signal(barrier, inc=1, device_id=device, device_id_type=pl.DeviceIdType.MESH)
    rep_copy = pltpu.make_async_copy(rep_hbm, rep, ls.at[0])
    mp_copy = pltpu.make_async_copy(mp_hbm, mp, ls.at[1])
    rep_copy.start()
    mp_copy.start()
    own_copy = pltpu.make_async_copy(bs_ref, gat.at[grp, core, beta, alpha], ls.at[2])
    own_copy.start()
    pl.semaphore_wait(barrier, len(greeted))

    def remote(src, dst, send_sem, recv_sem, device):
        return pltpu.make_async_remote_copy(
            src_ref=src, dst_ref=dst, send_sem=send_sem, recv_sem=recv_sem,
            device_id=device, device_id_type=pl.DeviceIdType.MESH)

    class Ring:
        def __init__(self, index, sign):
            self.index, self.sign = index, sign
            self.sent, self.done = [], 0
            self.coarse, self.idx, self.raw, self.compact = {}, {}, {}, {}

        def send(self, src, dst):
            k = len(self.sent)
            if k - self.done >= QUEUE:
                self.sent[self.done].wait_send()
                self.done += 1
            copy = remote(src, dst, zs.at[self.index, k], zr.at[self.index, k], z_device(self.sign))
            copy.start()
            self.sent.append(copy)
            return copy

        def drain(self):
            while self.done < len(self.sent):
                self.sent[self.done].wait_send()
                self.done += 1

        def coarse_hops(self):
            return half if self.index == 0 else half - 1

        def send_coarse(self, h):
            if h > self.coarse_hops():
                return
            source = group_at(-self.sign, h - 1)
            place = gat.at[source, core, beta, alpha]
            self.coarse[h] = self.send(bs_ref if h == 1 else place, place)

        def send_idx(self, h):
            src = v_ref if h == 1 else vbuf.at[self.index, h - 2]
            self.idx[h] = self.send(src, vbuf.at[self.index, h - 1])

        def send_raw(self, r):
            if r < CHUNKS:
                src = bp_ref.at[pl.ds(r * rows, rows), :]
            else:
                src = ring.at[self.index, r - CHUNKS]
            self.raw[r] = self.send(src, ring.at[self.index, r])

        def tail_rows(self, d):
            if d < half:
                return 0, block
            first = (slots - slots // 3) * MOST
            return (0, first) if self.index == 0 else (first, block - first)

        def send_compact(self, k):
            h, d = messages[k]
            _, count = self.tail_rows(d)
            if h == raw_hops + 1:
                src = dbuf.at[self.index, half - d, pl.ds(0, count)]
            else:
                before = messages.index((h - 1, d))
                self.compact[before].wait_recv()
                src = cbuf.at[self.index, before, pl.ds(0, count)]
            self.compact[k] = self.send(src, cbuf.at[self.index, k, pl.ds(0, count)])

    rings = [Ring(0, 1), Ring(1, -1)]

    def source_of(ring_, h):
        return group_at(-ring_.sign, h)

    def spread_copies(source, slot, phase):
        copies = []
        if phase == 0:
            place = gat.at[source, core, beta, alpha]
            for i in range(1, edge):
                copies.append(remote(place, place, xs.at[slot, 0, i - 1], xr.at[slot, 0, i - 1], a_device(i)))
        elif phase == 1:
            place = gat.at[source, core, beta]
            for i in range(1, edge):
                copies.append(remote(place, place, xs.at[slot, 1, i - 1], xr.at[slot, 1, i - 1], b_device(i)))
        else:
            place = gat.at[source, core]
            copies.append(remote(place, place, xs.at[slot, 2, 0], xr.at[mirror[slot], 2, 0], partner))
        return copies

    spread = {}

    def slot_of(index, h):
        return 0 if h == 0 else 2 * h - 1 + index

    mirror = {slot_of(i, h): slot_of(i if h == half else 1 - i, h) for h in range(1, half + 1) for i in range(2)}
    mirror[0] = 0

    def spread_step(slot, source, phase):
        if phase > 0:
            for copy in spread[mirror[slot] if phase == 3 else slot, phase - 1]:
                copy.wait_recv()
        if phase < 3:
            copies = spread_copies(source, slot, phase)
            for copy in copies:
                copy.start()
            spread[slot, phase] = copies

    out_copies = []
    scale = bs_ref.shape[1] ** (-0.5)

    def coarse_matmul(source):
        lhs = gat[source].reshape(2 * edge * edge * 8, bs_ref.shape[1])
        scores = lax.dot_general(lhs, rep[...], (((1,), (1,)), ((), ())), preferred_element_type=F32) * scale
        scores = scores.reshape(2, edge, edge, 8, scores.shape[-1])
        for b in range(edge):
            for a in range(edge):
                stage[source, b, a, 0] = scores[0, b, a].astype(BF)
                stage[source, a, b, 1] = scores[1, b, a].astype(BF)
        copy = pltpu.make_async_copy(stage.at[source], out_ref.at[source], os_.at[len(out_copies)])
        copy.start()
        out_copies.append(copy)

    def raw_rows(ring_, h):
        if h == 0:
            return bp_ref[...]
        return ring[ring_.index, pl.ds((h - 1) * CHUNKS, CHUNKS)].reshape(bins, width)

    def one_hot(targets, v):
        hit = (targets == v[0:1]) | (targets == v[1:2])
        return jnp.where(hit, 1.0, 0.0).astype(BF)

    def pick(targets, v, values):
        return jnp.dot(one_hot(targets, v), values, preferred_element_type=F32).astype(BF)

    order = [(1, 0)] + [(sign, h) for h in range(1, half) for sign in (1, -1)] + [(1, half)]

    def ring_of(sign):
        return core if sign == 1 else 1 - core

    def extract(ring_, h):
        k = 0 if ring_ is None else slot_of(ring_.index, h)
        targets = lax.broadcasted_iota(I32, (block, bins), 0) + block * grp
        v = v_ref[...] if ring_ is None else vbuf[ring_.index, h - 1]
        ext[k] = pick(targets, v, raw_rows(ring_, h))

    def compact(ring_):
        pieces = []
        for d in range(half, raw_hops, -1):
            first, count = ring_.tail_rows(d)
            dest = group_at(ring_.sign, d - raw_hops)
            pieces.append(lax.broadcasted_iota(I32, (count, bins), 0) + (block * dest + first))
        targets = jnp.concatenate(pieces, axis=0)
        picked = pick(targets, vbuf[ring_.index, raw_hops - 1], raw_rows(ring_, raw_hops))
        at = 0
        for d in range(half, raw_hops, -1):
            _, count = ring_.tail_rows(d)
            dbuf[ring_.index, half - d, pl.ds(0, count)] = picked[at:at + count]
            at += count

    def routed_rows(k, s):
        sign, h = order[k]
        if h <= raw_hops:
            at = 0 if h == 0 else 2 * h - 1 + ring_of(sign)
            return ext[at, pl.ds(s * MOST, MOST)]
        if h < half:
            return cbuf[ring_of(sign), messages.index((h, h)), pl.ds(s * MOST, MOST)]
        for each in rings:
            first, count = each.tail_rows(half)
            if first <= s * MOST < first + count:
                return cbuf[each.index, messages.index((half, half)), pl.ds(s * MOST - first, MOST)]

    per_batch = n // 2
    lanes = per_batch * MOST
    share = mp.shape[1] // m_all

    def fine_matmul(batch):
        for s in range(slots):
            rhs = jnp.concatenate([routed_rows(batch * per_batch + k, s) for k in range(per_batch)], axis=0)
            product = lax.dot_general(mp[s], rhs, (((1,), (1,)), ((), ())), preferred_element_type=F32)
            part[batch, :, s] = product.reshape(m_all, share, lanes)

    def reduce_copy(batch, i):
        to = lax.rem(mem + i, m_all)
        return remote(part.at[batch, to], red.at[batch, i - 1], rs.at[batch], rr.at[batch],
                      {"grp": grp, "mem": to})

    def reduce_start(batch):
        @pl.loop(1, m_all)
        def _(i):
            reduce_copy(batch, i).start()

    def all_reduced(batch, sem):
        whole = red.at[batch]
        return pltpu.make_async_copy(whole, whole, sem)

    returns = {}

    def reduce_finish(batch):
        all_reduced(batch, rr.at[batch]).wait()
        total = part[batch, mem] + jnp.sum(red[batch], axis=0)
        lane = lax.broadcasted_iota(I32, (share, lanes), 1)
        for k in range(per_batch):
            tile = jnp.zeros((share, lanes), F32)
            for s in range(slots):
                moved = pltpu.roll(total[s], (MOST * (s - k)) % lanes, 1)
                tile = jnp.where((lane >= MOST * s) & (lane < MOST * (s + 1)), moved, tile)
            at = batch * per_batch + k
            if at == 0:
                ret[at] = tile
            else:
                sums[at] = tile
        for k in range(per_batch):
            at = batch * per_batch + k
            sign, h = order[at]
            if at > 0:
                copy = remote(sums.at[at], ret.at[at], ts.at[at], tr.at[at],
                              {"grp": lax.rem(grp - sign * h + n, n), "mem": mem})
                copy.start()
                returns[at] = copy

    total_rounds = raw_hops * CHUNKS
    steps = {}

    def at_round(r, action):
        steps.setdefault(r, []).append(action)

    stride = max(1, total_rounds // half)
    for h in range(0, half + 1):
        for ring_ in rings:
            if h > ring_.coarse_hops() or (h == 0 and ring_.index == 1):
                continue
            k = slot_of(ring_.index, h)
            base = stride * h

            def arrive(ring_=ring_, h=h, k=k):
                if h > 0:
                    ring_.coarse[h].wait_recv()
                    if h < ring_.coarse_hops():
                        ring_.send_coarse(h + 1)
                else:
                    own_copy.wait()
                spread_step(k, source_of(ring_, h), 0)

            at_round(base, arrive)
            for phase in (1, 2, 3):
                at_round(base + stride * phase + phase,
                         functools.partial(spread_step, k, source_of(ring_, h), phase))

            def multiply(ring_=ring_, h=h):
                if h == 0:
                    rep_copy.wait()
                coarse_matmul(source_of(ring_, h))

            at_round(base + stride * 3 + 3, multiply)

    at_round(2, functools.partial(extract, None, 0))
    for h in range(1, raw_hops):
        for ring_ in rings:
            at_round((h + 1) * CHUNKS + ring_.index + 1, functools.partial(extract, ring_, h))

    for ring_ in rings:
        ring_.send_coarse(1)
        ring_.send_idx(1)
    for r in range(total_rounds):
        for ring_ in rings:
            if r >= CHUNKS:
                if r % CHUNKS == 0:
                    ring_.idx[r // CHUNKS].wait_recv()
                    ring_.send_idx(r // CHUNKS + 1)
                ring_.raw[r - CHUNKS].wait_recv()
            ring_.send_raw(r)
        for action in steps.pop(r, []):
            action()

    for ring_ in rings:
        ring_.idx[raw_hops].wait_recv()
        for r in range(total_rounds - CHUNKS, total_rounds):
            ring_.raw[r].wait_recv()
        compact(ring_)
        ring_.send_compact(0)

    first_batch = (half - raw_hops) + 1
    at_round(total_rounds + 1, functools.partial(extract, rings[0], raw_hops))
    at_round(total_rounds + 2, functools.partial(extract, rings[1], raw_hops))

    early = set()

    def begin_first():
        mp_copy.wait()
        for h in sorted({h for _, h in order[:per_batch] if h > raw_hops}):
            for ring_ in rings:
                ring_.compact[messages.index((h, h))].wait_recv()
                early.add(h)
        fine_matmul(0)
        reduce_start(0)

    at_round(total_rounds + first_batch + 1, begin_first)
    at_round(total_rounds + first_batch + 5, functools.partial(reduce_finish, 0))

    for k in range(0, len(messages)):
        for ring_ in rings:
            if k > 0:
                ring_.send_compact(k)
        for action in steps.pop(total_rounds + k, []):
            action()
    for r in sorted(steps):
        for action in steps[r]:
            action()

    for h in range(raw_hops + 1, half + 1):
        if h not in early:
            for ring_ in rings:
                ring_.compact[messages.index((h, h))].wait_recv()
    fine_matmul(1)
    reduce_start(1)
    for ring_ in rings:
        ring_.drain()
    for copies in spread.values():
        for copy in copies:
            copy.wait_send()
    for copy in out_copies:
        copy.wait()
    reduce_finish(1)
    for at in returns:
        returns[at].wait_recv()

    gathered = jnp.concatenate([ret[k] for k in range(n)], axis=1)
    high = gathered.astype(BF).astype(F32)
    rest = gathered - high
    middle = rest.astype(BF).astype(F32)
    low = rest - middle
    spare = jnp.zeros((-3 * share % 16, n * lanes), F32)
    lhs = jnp.concatenate([high, middle, low, spare], axis=0).astype(BF)
    q = lax.broadcasted_iota(I32, (lanes, bins), 0)
    targets = []
    for sign, h in order:
        owner = lax.rem(grp + sign * h + n, n)
        targets.append(jnp.where(q < block, q + block * owner, -1))
    targets = jnp.concatenate(targets, axis=0)
    for r in range(2):
        chosen = jnp.where(targets == v_ref[r:r + 1, :], 1.0, 0.0).astype(BF)
        got = jnp.dot(lhs, chosen, preferred_element_type=F32)
        fine_ref[r] = got[0:share] + got[share:2 * share] + got[2 * share:3 * share]

    for batch in range(2):
        all_reduced(batch, rs.at[batch]).wait()
    for at in returns:
        returns[at].wait_send()


def local(bin_sketch, rep_sketch, bin_profile, member_profile, bin_routes, owner_slot, cluster_sizes, raw=RAW):
    bins, width = bin_profile.shape
    slots, members, _ = member_profile.shape
    bin_dev, w = bin_sketch.shape
    reps = rep_sketch.shape[0]
    n, m_all = lax.axis_size("grp"), lax.axis_size("mem")
    edge = int(round((m_all // 2) ** 0.5))
    half = n // 2
    share = members // m_all
    cluster_total = owner_slot.shape[0]
    block = slots * MOST
    lanes = half * MOST
    messages = compact_list(half, raw)

    routes = bin_routes.T.reshape(-1)
    ids = jnp.arange(cluster_total, dtype=I32)
    hit = (routes[:, None] == ids[None, :]).astype(I32)
    storage = jnp.sum(hit * owner_slot[None, :], axis=1)
    size = jnp.sum(hit * cluster_sizes[None, :], axis=1)
    rank = jnp.sum((jnp.cumsum(hit, axis=0) - hit) * hit, axis=1)
    index = (storage * MOST + rank).reshape(2, bins)
    v = jnp.concatenate([index, jnp.full((6, bins), -1, I32)], axis=0)

    z_sends = half + raw + raw * CHUNKS + len(messages)
    cfg = {"n": n, "m": m_all, "edge": edge, "raw": raw}
    vmem = pl.BlockSpec(memory_space=pltpu.VMEM)
    hbm = pl.BlockSpec(memory_space=pl.ANY)
    dma = pltpu.SemaphoreType.DMA
    coarse, fine = pl.pallas_call(
        functools.partial(screen, cfg),
        out_shape=(
            jax.ShapeDtypeStruct((n, edge, edge, 2, bin_dev, reps), BF),
            jax.ShapeDtypeStruct((2, share, bins), F32),
        ),
        in_specs=[vmem, hbm, vmem, hbm, vmem],
        out_specs=(hbm, vmem),
        scratch_shapes=[
            pltpu.VMEM((2, raw * CHUNKS, bins // CHUNKS, width), BF),
            pltpu.VMEM((2, raw, 8, bins), I32),
            pltpu.VMEM((2, len(messages), block, width), BF),
            pltpu.VMEM((2, half - raw, block, width), BF),
            pltpu.VMEM((2 * raw + 1, block, width), BF),
            pltpu.VMEM((n, 2, edge, edge, bin_dev, w), BF),
            pltpu.VMEM((reps, w), BF),
            pltpu.VMEM((slots, members, width), BF),
            pltpu.VMEM((n, edge, edge, 2, bin_dev, reps), BF),
            pltpu.VMEM((2, m_all, slots, share, lanes), F32),
            pltpu.VMEM((2, m_all - 1, slots, share, lanes), F32),
            pltpu.VMEM((n, share, lanes), F32),
            pltpu.VMEM((n, share, lanes), F32),
            dma((2, z_sends)), dma((2, z_sends)),
            dma((n, 3, edge - 1)), dma((n, 3, edge - 1)),
            dma((2,)), dma((2,)),
            dma((n,)), dma((n,)),
            dma((3,)), dma((n,)),
        ],
        compiler_params=pltpu.CompilerParams(
            collective_id=0, has_side_effects=True, vmem_limit_bytes=56 * 1024 * 1024),
    )(bin_sketch, rep_sketch, bin_profile, member_profile, v)
    coarse = coarse.reshape(n * m_all * bin_dev, reps)
    column = lax.axis_index("mem") * share + jnp.arange(share, dtype=I32)
    live = column[None, :, None] < size.reshape(2, 1, bins)
    scaled = jnp.where(live, fine * (width * m_all) ** (-0.5), 0.0)
    return (coarse, scaled.transpose(2, 0, 1))


def solution(mesh):
    return jax.shard_map(
        local,
        mesh=mesh,
        in_specs=(
            P(("grp", "mem"), None),
            P(("grp", "mem"), None),
            P("grp", "mem"),
            P("grp", None, "mem"),
            P("grp", None),
            P(),
            P(),
        ),
        out_specs=(P(None, ("grp", "mem")), P("grp", None, "mem")),
        check_vma=False,
    )
```

```python
import functools

import jax
import jax.numpy as jnp
from jax import lax
from jax.experimental import pallas as pl
from jax.experimental.pallas import tpu as pltpu
from jax.sharding import PartitionSpec as P

MOST = 16
RAW = 3
CHUNKS = 8
QUEUE = 3
LAG = 2
BF = jnp.bfloat16
F32 = jnp.float32
I32 = jnp.int32


def compact_list(half, raw):
    left = [(h, d) for h in range(raw + 1, half + 1) for d in range(half, h - 1, -1)]
    order = []
    while left:
        ready = [p for p in left if p[0] == raw + 1 or (p[0] - 1, p[1]) in order[: max(0, len(order) - LAG)]]
        if not ready:
            ready = [p for p in left if p[0] == raw + 1 or (p[0] - 1, p[1]) in order]
        best = max(ready, key=lambda p: (p[1], -p[0]))
        order.append(best)
        left.remove(best)
    return order


def screen(cfg, bs_ref, rep_hbm, bp_hbm, mp_hbm, routes_ref, owner_ref, size_ref, out_ref, fine_ref, *scratch):
    n, m_all, edge, raw_hops = cfg["n"], cfg["m"], cfg["edge"], cfg["raw"]
    (bp_ref, v_ref, ring, vbuf, cbuf, dbuf, ext, gat, rep, mp, part, red, sums, ret,
     zs, zr, xs, xr, rs, rr, ts, tr, ls) = scratch
    half = n // 2
    messages = compact_list(half, raw_hops)
    grp = lax.axis_index("grp")
    mem = lax.axis_index("mem")
    core = lax.rem(mem, 2)
    sigma = 1 - 2 * core
    chip = mem // 2
    y, x = chip // edge, lax.rem(chip, edge)
    alpha = jnp.where(core == 0, x, y)
    beta = jnp.where(core == 0, y, x)
    bins = bp_ref.shape[0]
    width = bp_ref.shape[1]
    rows = bins // CHUNKS
    slots = mp.shape[0]
    block = slots * MOST

    def group_at(sign, distance):
        return lax.rem(grp + sigma * (sign * distance) + n, n)

    def z_device(sign):
        return {"grp": group_at(sign, 1), "mem": mem}

    def member_at(a, b):
        yy = jnp.where(core == 0, b, a)
        xx = jnp.where(core == 0, a, b)
        return (yy * edge + xx) * 2 + core

    def a_device(i):
        return {"grp": grp, "mem": member_at(lax.rem(alpha + i, edge), beta)}

    def b_device(i):
        return {"grp": grp, "mem": member_at(alpha, lax.rem(beta + i, edge))}

    partner = {"grp": grp, "mem": mem + sigma}

    greeted = [z_device(1), z_device(-1), partner]
    greeted += [a_device(i) for i in range(1, edge)] + [b_device(i) for i in range(1, edge)]
    barrier = pltpu.get_barrier_semaphore()
    for device in greeted:
        pl.semaphore_signal(barrier, inc=1, device_id=device, device_id_type=pl.DeviceIdType.MESH)
    rep_copy = pltpu.make_async_copy(rep_hbm, rep, ls.at[0])
    mp_copy = pltpu.make_async_copy(mp_hbm, mp, ls.at[1])
    own_copy = pltpu.make_async_copy(bs_ref, gat.at[grp, core, beta, alpha], ls.at[2])
    own_copy.start()
    bp_copy = pltpu.make_async_copy(bp_hbm, bp_ref, ls.at[3])
    bp_copy.start()
    rep_copy.start()
    mp_copy.start()
    pl.semaphore_wait(barrier, len(greeted))

    def remote(src, dst, send_sem, recv_sem, device):
        return pltpu.make_async_remote_copy(
            src_ref=src, dst_ref=dst, send_sem=send_sem, recv_sem=recv_sem,
            device_id=device, device_id_type=pl.DeviceIdType.MESH)

    class Ring:
        def __init__(self, index, sign):
            self.index, self.sign = index, sign
            self.sent, self.done = [], 0
            self.coarse, self.idx, self.raw, self.compact = {}, {}, {}, {}

        def send(self, src, dst):
            k = len(self.sent)
            if k - self.done >= QUEUE:
                self.sent[self.done].wait_send()
                self.done += 1
            copy = remote(src, dst, zs.at[self.index, k], zr.at[self.index, k], z_device(self.sign))
            copy.start()
            self.sent.append(copy)
            return copy

        def drain(self):
            while self.done < len(self.sent):
                self.sent[self.done].wait_send()
                self.done += 1

        def coarse_hops(self):
            return half if self.index == 0 else half - 1

        def send_coarse(self, h):
            if h > self.coarse_hops():
                return
            source = group_at(-self.sign, h - 1)
            place = gat.at[source, core, beta, alpha]
            self.coarse[h] = self.send(bs_ref if h == 1 else place, place)

        def send_idx(self, h):
            src = v_ref if h == 1 else vbuf.at[self.index, h - 2]
            self.idx[h] = self.send(src, vbuf.at[self.index, h - 1])

        def send_raw(self, r):
            if r < CHUNKS:
                src = bp_hbm.at[pl.ds(r * rows, rows), :]
            else:
                src = ring.at[self.index, r - CHUNKS]
            self.raw[r] = self.send(src, ring.at[self.index, r])

        def tail_rows(self, d):
            if d < half:
                return 0, block
            first = (slots - slots // 3) * MOST
            return (0, first) if self.index == 0 else (first, block - first)

        def send_compact(self, k):
            h, d = messages[k]
            _, count = self.tail_rows(d)
            if h == raw_hops + 1:
                src = dbuf.at[self.index, half - d, pl.ds(0, count)]
            else:
                before = messages.index((h - 1, d))
                self.compact[before].wait_recv()
                src = cbuf.at[self.index, before, pl.ds(0, count)]
            self.compact[k] = self.send(src, cbuf.at[self.index, k, pl.ds(0, count)])

    rings = [Ring(0, 1), Ring(1, -1)]

    def route():
        clusters = owner_ref.shape[1]
        routes = jnp.concatenate([routes_ref[0:1], routes_ref[1:2]], axis=1)
        hit = jnp.where(lax.broadcasted_iota(I32, (clusters, 2 * bins), 0) == routes, 1.0, 0.0)
        before = (lax.broadcasted_iota(I32, (2 * bins, 2 * bins), 0)
                  < lax.broadcasted_iota(I32, (2 * bins, 2 * bins), 1))
        earlier = jnp.dot(hit.astype(BF), jnp.where(before, 1.0, 0.0).astype(BF), preferred_element_type=F32)
        rank = jnp.sum(hit * earlier, axis=0, keepdims=True)
        table = jnp.concatenate([owner_ref[...].astype(F32), size_ref[...].astype(F32),
                                 jnp.zeros((14, clusters), F32)], axis=0)
        looked = jnp.dot(table.astype(BF), hit.astype(BF), preferred_element_type=F32)
        index = (looked[0:1] * MOST + rank).astype(I32)
        v_ref[...] = jnp.concatenate(
            [index[:, :bins], index[:, bins:], jnp.full((6, bins), -1, I32)], axis=0)
        return looked[1:2]

    def source_of(ring_, h):
        return group_at(-ring_.sign, h)

    def spread_copies(source, slot, phase):
        copies = []
        if phase == 0:
            place = gat.at[source, core, beta, alpha]
            for i in range(1, edge):
                copies.append(remote(place, place, xs.at[slot, 0, i - 1], xr.at[slot, 0, i - 1], a_device(i)))
        elif phase == 1:
            place = gat.at[source, core, beta]
            for i in range(1, edge):
                copies.append(remote(place, place, xs.at[slot, 1, i - 1], xr.at[slot, 1, i - 1], b_device(i)))
        else:
            place = gat.at[source, core]
            copies.append(remote(place, place, xs.at[slot, 2, 0], xr.at[mirror[slot], 2, 0], partner))
        return copies

    spread = {}

    def slot_of(index, h):
        return 0 if h == 0 else 2 * h - 1 + index

    mirror = {slot_of(i, h): slot_of(i if h == half else 1 - i, h) for h in range(1, half + 1) for i in range(2)}
    mirror[0] = 0

    def spread_step(slot, source, phase):
        if phase > 0:
            for copy in spread[mirror[slot] if phase == 3 else slot, phase - 1]:
                copy.wait_recv()
        if phase < 3:
            copies = spread_copies(source, slot, phase)
            for copy in copies:
                copy.start()
            spread[slot, phase] = copies

    scale = bs_ref.shape[1] ** (-0.5)

    def coarse_matmul(source):
        lhs = gat[source].reshape(2 * edge * edge * 8, bs_ref.shape[1])
        scores = lax.dot_general(lhs, rep[...], (((1,), (1,)), ((), ())), preferred_element_type=F32) * scale
        scores = scores.reshape(2, edge, edge, 8, scores.shape[-1])
        for b in range(edge):
            for a in range(edge):
                out_ref[source, b, a, 0] = scores[0, b, a].astype(BF)
                out_ref[source, a, b, 1] = scores[1, b, a].astype(BF)

    def raw_rows(ring_, h):
        if h == 0:
            return bp_ref[...]
        return ring[ring_.index, pl.ds((h - 1) * CHUNKS, CHUNKS)].reshape(bins, width)

    def one_hot(targets, v):
        hit = (targets == v[0:1]) | (targets == v[1:2])
        return jnp.where(hit, 1.0, 0.0).astype(BF)

    def pick(targets, v, values):
        return jnp.dot(one_hot(targets, v), values, preferred_element_type=F32).astype(BF)

    split = (half + raw_hops) // 2
    every = [(1, 0)] + [(sign, h) for h in range(1, half) for sign in (1, -1)] + [(1, half)]
    batches = [[e for e in every if e[1] <= raw_hops], [e for e in every if e[1] > split],
               [e for e in every if raw_hops < e[1] <= split]]
    order = sum(batches, [])
    base_of = [0, len(batches[0]), len(batches[0]) + len(batches[1])]

    def ring_of(sign):
        return core if sign == 1 else 1 - core

    def extract(ring_, h):
        k = 0 if ring_ is None else slot_of(ring_.index, h)
        targets = lax.broadcasted_iota(I32, (block, bins), 0) + block * grp
        v = v_ref[...] if ring_ is None else vbuf[ring_.index, h - 1]
        ext[k] = pick(targets, v, raw_rows(ring_, h))

    def compact(ring_, distances):
        pieces = []
        for d in distances:
            first, count = ring_.tail_rows(d)
            dest = group_at(ring_.sign, d - raw_hops)
            pieces.append(lax.broadcasted_iota(I32, (count, bins), 0) + (block * dest + first))
        targets = jnp.concatenate(pieces, axis=0)
        picked = pick(targets, vbuf[ring_.index, raw_hops - 1], raw_rows(ring_, raw_hops))
        at = 0
        for d in distances:
            _, count = ring_.tail_rows(d)
            dbuf[ring_.index, half - d, pl.ds(0, count)] = picked[at:at + count]
            at += count

    def routed_rows(k, s):
        sign, h = k
        if h <= raw_hops:
            at = 0 if h == 0 else 2 * h - 1 + ring_of(sign)
            return ext[at, pl.ds(s * MOST, MOST)]
        if h < half:
            return cbuf[ring_of(sign), messages.index((h, h)), pl.ds(s * MOST, MOST)]
        for each in rings:
            first, count = each.tail_rows(half)
            if first <= s * MOST < first + count:
                return cbuf[each.index, messages.index((half, half)), pl.ds(s * MOST - first, MOST)]

    per_tile = half
    lanes = per_tile * MOST
    share = mp.shape[1] // m_all

    def pieces_of(batch):
        return [(e, s) for s in range(slots) for e in batches[batch]]

    def tiles_of(batch):
        return -(-len(pieces_of(batch)) // per_tile)

    def fine_matmul(batch):
        pieces = pieces_of(batch)
        for t in range(tiles_of(batch)):
            here = pieces[t * per_tile:(t + 1) * per_tile]
            total = None
            for s in sorted({piece[1] for piece in here}):
                parts = [routed_rows(e, s) if slot == s else jnp.zeros((MOST, width), BF) for e, slot in here]
                parts += [jnp.zeros((MOST, width), BF)] * (per_tile - len(here))
                product = lax.dot_general(mp[s], jnp.concatenate(parts, axis=0), (((1,), (1,)), ((), ())),
                                          preferred_element_type=F32)
                total = product if total is None else total + product
            part[batch, :, t] = total.reshape(m_all, share, lanes)

    def reduce_copy(batch, i):
        to = lax.rem(mem + i, m_all)
        count = tiles_of(batch)
        return remote(part.at[batch, to, pl.ds(0, count)], red.at[batch, i - 1, pl.ds(0, count)],
                      rs.at[batch], rr.at[batch], {"grp": grp, "mem": to})

    def reduce_start(batch):
        @pl.loop(1, m_all)
        def _(i):
            reduce_copy(batch, i).start()

    def all_reduced(batch, sem):
        whole = red.at[batch, :, pl.ds(0, tiles_of(batch))]
        return pltpu.make_async_copy(whole, whole, sem)

    returns = {}

    def reduce_finish(batch):
        all_reduced(batch, rr.at[batch]).wait()
        count = tiles_of(batch)
        total = part[batch, mem, pl.ds(0, count)] + jnp.sum(red[batch, :, pl.ds(0, count)], axis=0)
        lane = lax.broadcasted_iota(I32, (share, lanes), 1)
        pieces = pieces_of(batch)
        for k, entry in enumerate(batches[batch]):
            tile = jnp.zeros((share, lanes), F32)
            for s in range(slots):
                p = pieces.index((entry, s))
                moved = pltpu.roll(total[p // per_tile], (MOST * (s - p % per_tile)) % lanes, 1)
                tile = jnp.where((lane >= MOST * s) & (lane < MOST * (s + 1)), moved, tile)
            at = base_of[batch] + k
            if at == 0:
                ret[at] = tile
            else:
                sums[at] = tile
        for k, (sign, h) in enumerate(batches[batch]):
            at = base_of[batch] + k
            if at > 0:
                copy = remote(sums.at[at], ret.at[at], ts.at[at], tr.at[at],
                              {"grp": lax.rem(grp - sign * h + n, n), "mem": mem})
                copy.start()
                returns[at] = copy

    total_rounds = raw_hops * CHUNKS
    steps = {}

    def at_round(r, action):
        steps.setdefault(r, []).append(action)

    stride = max(1, total_rounds // half)
    for h in range(0, half + 1):
        for ring_ in rings:
            if h > ring_.coarse_hops() or (h == 0 and ring_.index == 1):
                continue
            k = slot_of(ring_.index, h)
            base = stride * h

            def arrive(ring_=ring_, h=h, k=k):
                if h > 0:
                    ring_.coarse[h].wait_recv()
                    if h < ring_.coarse_hops():
                        ring_.send_coarse(h + 1)
                else:
                    own_copy.wait()
                spread_step(k, source_of(ring_, h), 0)

            at_round(base, arrive)
            for phase in (1, 2, 3):
                at_round(base + stride * phase + phase,
                         functools.partial(spread_step, k, source_of(ring_, h), phase))

            def multiply(ring_=ring_, h=h):
                if h == 0:
                    rep_copy.wait()
                coarse_matmul(source_of(ring_, h))

            at_round(base + stride * 3 + 3, multiply)

    at_round(2, functools.partial(extract, None, 0))
    for h in range(1, raw_hops):
        for ring_ in rings:
            at_round((h + 1) * CHUNKS + ring_.index + 1, functools.partial(extract, ring_, h))

    for ring_ in rings:
        ring_.send_coarse(1)
    sizes = []

    def begin_routes():
        sizes.append(route())
        for ring_ in rings:
            ring_.send_idx(1)
        bp_copy.wait()

    at_round(1, begin_routes)
    steps[1] = steps[1][-1:] + steps[1][:-1]
    for r in range(total_rounds):
        for ring_ in rings:
            if r >= CHUNKS:
                if r % CHUNKS == 0:
                    ring_.idx[r // CHUNKS].wait_recv()
                    ring_.send_idx(r // CHUNKS + 1)
                ring_.raw[r - CHUNKS].wait_recv()
            ring_.send_raw(r)
        for action in steps.pop(r, []):
            action()

    for ring_ in rings:
        ring_.idx[raw_hops].wait_recv()
        for r in range(total_rounds - CHUNKS, total_rounds):
            ring_.raw[r].wait_recv()
        compact(ring_, range(half, split, -1))
        ring_.send_compact(0)

    for ring_ in rings:
        at_round(total_rounds + 1, functools.partial(compact, ring_, range(split, raw_hops, -1)))
    at_round(total_rounds + 2, functools.partial(extract, rings[0], raw_hops))
    at_round(total_rounds + 2, functools.partial(extract, rings[1], raw_hops))

    def begin_first():
        mp_copy.wait()
        fine_matmul(0)
        reduce_start(0)

    at_round(total_rounds + 3, begin_first)
    at_round(total_rounds + 9, functools.partial(reduce_finish, 0))

    for k in range(0, len(messages)):
        for ring_ in rings:
            if k > 0:
                ring_.send_compact(k)
        for action in steps.pop(total_rounds + k, []):
            action()
    for r in sorted(steps):
        for action in steps[r]:
            action()

    for batch in (1, 2):
        for h in sorted({h for _, h in batches[batch]}):
            for ring_ in rings:
                ring_.compact[messages.index((h, h))].wait_recv()
        fine_matmul(batch)
        reduce_start(batch)
    for ring_ in rings:
        ring_.drain()
    for copies in spread.values():
        for copy in copies:
            copy.wait_send()
    reduce_finish(1)
    reduce_finish(2)
    for at in returns:
        returns[at].wait_recv()

    gathered = jnp.concatenate([ret[k] for k in range(n)], axis=1)
    high = gathered.astype(BF).astype(F32)
    rest = gathered - high
    middle = rest.astype(BF).astype(F32)
    low = rest - middle
    spare = jnp.zeros((-3 * share % 16, n * lanes), F32)
    lhs = jnp.concatenate([high, middle, low, spare], axis=0).astype(BF)
    q = lax.broadcasted_iota(I32, (lanes, bins), 0)
    targets = []
    for sign, h in order:
        owner = lax.rem(grp + sign * h + n, n)
        targets.append(jnp.where(q < block, q + block * owner, -1))
    targets = jnp.concatenate(targets, axis=0)
    for r in range(2):
        chosen = jnp.where(targets == v_ref[r:r + 1, :], 1.0, 0.0).astype(BF)
        got = jnp.dot(lhs, chosen, preferred_element_type=F32)
        whole = got[0:share] + got[share:2 * share] + got[2 * share:3 * share]
        column = (lax.broadcasted_iota(I32, (share, bins), 0) + mem * share).astype(F32)
        live = column < sizes[0][:, r * bins:(r + 1) * bins]
        fine_ref[r] = jnp.where(live, whole * (width * m_all) ** (-0.5), 0.0)

    for batch in range(3):
        all_reduced(batch, rs.at[batch]).wait()
    for at in returns:
        returns[at].wait_send()


def local(bin_sketch, rep_sketch, bin_profile, member_profile, bin_routes, owner_slot, cluster_sizes, raw=RAW):
    bins, width = bin_profile.shape
    slots, members, _ = member_profile.shape
    bin_dev, w = bin_sketch.shape
    reps = rep_sketch.shape[0]
    n, m_all = lax.axis_size("grp"), lax.axis_size("mem")
    edge = int(round((m_all // 2) ** 0.5))
    half = n // 2
    share = members // m_all
    cluster_total = owner_slot.shape[0]
    block = slots * MOST
    lanes = half * MOST
    messages = compact_list(half, raw)

    z_sends = half + raw + raw * CHUNKS + len(messages)
    cfg = {"n": n, "m": m_all, "edge": edge, "raw": raw}
    vmem = pl.BlockSpec(memory_space=pltpu.VMEM)
    hbm = pl.BlockSpec(memory_space=pltpu.HBM)
    dma = pltpu.SemaphoreType.DMA
    coarse, fine = pl.pallas_call(
        functools.partial(screen, cfg),
        out_shape=(
            pltpu.VMEM((n, edge, edge, 2, bin_dev, reps), BF),
            pltpu.VMEM((2, share, bins), F32),
        ),
        in_specs=[hbm, hbm, hbm, hbm, vmem, vmem, vmem],
        out_specs=(vmem, vmem),
        scratch_shapes=[
            pltpu.VMEM((bins, width), BF),
            pltpu.VMEM((8, bins), I32),
            pltpu.VMEM((2, raw * CHUNKS, bins // CHUNKS, width), BF),
            pltpu.VMEM((2, raw, 8, bins), I32),
            pltpu.VMEM((2, len(messages), block, width), BF),
            pltpu.VMEM((2, half - raw, block, width), BF),
            pltpu.VMEM((2 * raw + 1, block, width), BF),
            pltpu.VMEM((n, 2, edge, edge, bin_dev, w), BF),
            pltpu.VMEM((reps, w), BF),
            pltpu.VMEM((slots, members, width), BF),
            pltpu.VMEM((3, m_all, slots, share, lanes), F32),
            pltpu.VMEM((3, m_all - 1, slots, share, lanes), F32),
            pltpu.VMEM((n, share, lanes), F32),
            pltpu.VMEM((n, share, lanes), F32),
            dma((2, z_sends)), dma((2, z_sends)),
            dma((n, 3, edge - 1)), dma((n, 3, edge - 1)),
            dma((3,)), dma((3,)),
            dma((n,)), dma((n,)),
            dma((4,)),
        ],
        compiler_params=pltpu.CompilerParams(
            collective_id=0, has_side_effects=True, vmem_limit_bytes=64749568),
    )(bin_sketch, rep_sketch, bin_profile, member_profile, bin_routes.T, owner_slot[None], cluster_sizes[None])
    return (coarse.reshape(n * m_all * bin_dev, reps), fine.transpose(2, 0, 1))


def solution(mesh):
    return jax.shard_map(
        local,
        mesh=mesh,
        in_specs=(
            P(("grp", "mem"), None),
            P(("grp", "mem"), None),
            P("grp", "mem"),
            P("grp", None, "mem"),
            P("grp", None),
            P(),
            P(),
        ),
        out_specs=(P(None, ("grp", "mem")), P("grp", None, "mem")),
        check_vma=False,
    )
```

```python
import functools

import jax
import jax.numpy as jnp
from jax import lax
from jax.experimental import pallas as pl
from jax.experimental.pallas import tpu as pltpu
from jax.sharding import PartitionSpec as P

MOST = 16
RAW = 3
CHUNKS = 8
QUEUE = 3
LAG = 2
BF = jnp.bfloat16
F32 = jnp.float32
I32 = jnp.int32


def compact_list(half, raw):
    left = [(h, d) for h in range(raw + 1, half + 1) for d in range(half, h - 1, -1)]
    if (half, raw) == (8, 3):
        return [(4, 8), (4, 7), (4, 6), (5, 8), (5, 7), (4, 5), (6, 8), (6, 7), (5, 6), (7, 8), (7, 7), (6, 6),
                (8, 8), (5, 5), (4, 4)]
    order = []
    while left:
        ready = [p for p in left if p[0] == raw + 1 or (p[0] - 1, p[1]) in order[: max(0, len(order) - LAG)]]
        if not ready:
            ready = [p for p in left if p[0] == raw + 1 or (p[0] - 1, p[1]) in order]
        best = max(ready, key=lambda p: (p[1], -p[0]))
        order.append(best)
        left.remove(best)
    return order


def screen(cfg, bs_ref, rep_hbm, bp_hbm, mp_hbm, routes_ref, owner_ref, size_ref, out_ref, fine_ref, *scratch):
    n, m_all, edge, raw_hops = cfg["n"], cfg["m"], cfg["edge"], cfg["raw"]
    (bp_ref, v_ref, ring, vbuf, cbuf, dbuf, ext, gat, rep, mp, part, red, sums, ret,
     zs, zr, xs, xr, rs, rr, ts, tr, ls) = scratch
    half = n // 2
    messages = compact_list(half, raw_hops)
    grp = lax.axis_index("grp")
    mem = lax.axis_index("mem")
    core = lax.rem(mem, 2)
    sigma = 1 - 2 * core
    chip = mem // 2
    y, x = chip // edge, lax.rem(chip, edge)
    alpha = jnp.where(core == 0, x, y)
    beta = jnp.where(core == 0, y, x)
    bins = bp_ref.shape[0]
    width = bp_ref.shape[1]
    rows = bins // CHUNKS
    slots = mp.shape[0]
    block = slots * MOST

    def group_at(sign, distance):
        return lax.rem(grp + sigma * (sign * distance) + n, n)

    def z_device(sign):
        return {"grp": group_at(sign, 1), "mem": mem}

    def member_at(a, b):
        yy = jnp.where(core == 0, b, a)
        xx = jnp.where(core == 0, a, b)
        return (yy * edge + xx) * 2 + core

    def a_device(i):
        return {"grp": grp, "mem": member_at(lax.rem(alpha + i, edge), beta)}

    def b_device(i):
        return {"grp": grp, "mem": member_at(alpha, lax.rem(beta + i, edge))}

    partner = {"grp": grp, "mem": mem + sigma}

    greeted = [z_device(1), z_device(-1), partner]
    greeted += [a_device(i) for i in range(1, edge)] + [b_device(i) for i in range(1, edge)]
    barrier = pltpu.get_barrier_semaphore()
    for device in greeted:
        pl.semaphore_signal(barrier, inc=1, device_id=device, device_id_type=pl.DeviceIdType.MESH)
    rep_copy = pltpu.make_async_copy(rep_hbm, rep, ls.at[0])
    mp_copy = pltpu.make_async_copy(mp_hbm, mp, ls.at[1])
    own_copy = pltpu.make_async_copy(bs_ref, gat.at[grp, core, beta, alpha], ls.at[2])
    own_copy.start()
    bp_copy = pltpu.make_async_copy(bp_hbm, bp_ref, ls.at[3])
    bp_copy.start()
    rep_copy.start()
    mp_copy.start()
    pl.semaphore_wait(barrier, len(greeted))

    def remote(src, dst, send_sem, recv_sem, device):
        return pltpu.make_async_remote_copy(
            src_ref=src, dst_ref=dst, send_sem=send_sem, recv_sem=recv_sem,
            device_id=device, device_id_type=pl.DeviceIdType.MESH)

    class Ring:
        def __init__(self, index, sign):
            self.index, self.sign = index, sign
            self.sent, self.done = [], 0
            self.coarse, self.idx, self.raw, self.compact = {}, {}, {}, {}

        def send(self, src, dst):
            k = len(self.sent)
            if k - self.done >= QUEUE:
                self.sent[self.done].wait_send()
                self.done += 1
            copy = remote(src, dst, zs.at[self.index, k % QUEUE], zr.at[self.index, k], z_device(self.sign))
            copy.start()
            self.sent.append(copy)
            return copy

        def drain(self):
            while self.done < len(self.sent):
                self.sent[self.done].wait_send()
                self.done += 1

        def coarse_hops(self):
            return half if self.index == 0 else half - 1

        def send_coarse(self, h):
            if h > self.coarse_hops():
                return
            source = group_at(-self.sign, h - 1)
            place = gat.at[source, core, beta, alpha]
            self.coarse[h] = self.send(bs_ref if h == 1 else place, place)

        def send_idx(self, h):
            src = v_ref if h == 1 else vbuf.at[self.index, h - 2]
            self.idx[h] = self.send(src, vbuf.at[self.index, h - 1])

        def send_raw(self, r):
            if r < CHUNKS:
                src = bp_hbm.at[pl.ds(r * rows, rows), :]
            else:
                src = ring.at[self.index, r - CHUNKS]
            self.raw[r] = self.send(src, ring.at[self.index, r])

        def tail_rows(self, d):
            if d < half:
                return 0, block
            first = (slots - slots // 3) * MOST
            return (0, first) if self.index == 0 else (first, block - first)

        def send_compact(self, k):
            h, d = messages[k]
            _, count = self.tail_rows(d)
            if h == raw_hops + 1:
                src = dbuf.at[self.index, half - d, pl.ds(0, count)]
            else:
                before = messages.index((h - 1, d))
                self.compact[before].wait_recv()
                src = cbuf.at[self.index, before, pl.ds(0, count)]
            self.compact[k] = self.send(src, cbuf.at[self.index, k, pl.ds(0, count)])

    rings = [Ring(0, 1), Ring(1, -1)]

    def route():
        clusters = owner_ref.shape[1]
        routes = jnp.concatenate([routes_ref[0:1], routes_ref[1:2]], axis=1)
        hit = jnp.where(lax.broadcasted_iota(I32, (clusters, 2 * bins), 0) == routes, 1.0, 0.0)
        before = (lax.broadcasted_iota(I32, (2 * bins, 2 * bins), 0)
                  < lax.broadcasted_iota(I32, (2 * bins, 2 * bins), 1))
        earlier = jnp.dot(hit.astype(BF), jnp.where(before, 1.0, 0.0).astype(BF), preferred_element_type=F32)
        rank = jnp.sum(hit * earlier, axis=0, keepdims=True)
        table = jnp.concatenate([owner_ref[...].astype(F32), size_ref[...].astype(F32),
                                 jnp.zeros((14, clusters), F32)], axis=0)
        looked = jnp.dot(table.astype(BF), hit.astype(BF), preferred_element_type=F32)
        index = (looked[0:1] * MOST + rank).astype(I32)
        v_ref[...] = jnp.concatenate(
            [index[:, :bins], index[:, bins:], jnp.full((6, bins), -1, I32)], axis=0)
        return looked[1:2]

    def source_of(ring_, h):
        return group_at(-ring_.sign, h)

    def spread_copies(source, slot, phase):
        copies = []
        if phase == 0:
            place = gat.at[source, core, beta, alpha]
            for i in range(1, edge):
                copies.append(remote(place, place, xs.at[0], xr.at[slot, 0], a_device(i)))
        elif phase == 1:
            place = gat.at[source, core, beta]
            for i in range(1, edge):
                copies.append(remote(place, place, xs.at[1], xr.at[slot, 1], b_device(i)))
        else:
            place = gat.at[source, core]
            copies.append(remote(place, place, xs.at[2], xr.at[mirror[slot], 2], partner))
        return copies

    def bytes_of(phase, planes, sem):
        whole = (gat.at[pl.ds(0, planes), 0, 0, pl.ds(0, edge - 1)],
                 gat.at[pl.ds(0, planes), 0, pl.ds(0, edge - 1)],
                 gat.at[pl.ds(0, planes), 0])[phase]
        return pltpu.make_async_copy(whole, whole, sem)

    def slot_of(index, h):
        return 0 if h == 0 else 2 * h - 1 + index

    mirror = {slot_of(i, h): slot_of(i if h == half else 1 - i, h) for h in range(1, half + 1) for i in range(2)}
    mirror[0] = 0

    def spread_step(slot, source, phase):
        if phase > 0:
            bytes_of(phase - 1, 1, xr.at[slot, phase - 1]).wait()
        if phase < 3:
            for copy in spread_copies(source, slot, phase):
                copy.start()

    scale = bs_ref.shape[1] ** (-0.5)

    def coarse_matmul(source):
        lhs = gat[source].reshape(2 * edge * edge * 8, bs_ref.shape[1])
        scores = lax.dot_general(lhs, rep[...], (((1,), (1,)), ((), ())), preferred_element_type=F32) * scale
        scores = scores.reshape(2, edge, edge, 8, scores.shape[-1])
        for b in range(edge):
            for a in range(edge):
                out_ref[source, b, a, 0] = scores[0, b, a].astype(BF)
                out_ref[source, a, b, 1] = scores[1, b, a].astype(BF)

    def raw_rows(ring_, h):
        if h == 0:
            return bp_ref[...]
        return ring[ring_.index, pl.ds((h - 1) * CHUNKS, CHUNKS)].reshape(bins, width)

    def one_hot(targets, v):
        hit = (targets == v[0:1]) | (targets == v[1:2])
        return jnp.where(hit, 1.0, 0.0).astype(BF)

    def pick(targets, v, values):
        return jnp.dot(one_hot(targets, v), values, preferred_element_type=F32).astype(BF)

    split = (half + raw_hops) // 2
    every = [(1, 0)] + [(sign, h) for h in range(1, half) for sign in (1, -1)] + [(1, half)]
    batches = [[e for e in every if e[1] <= raw_hops], [e for e in every if e[1] > split]]
    batches += [[e for e in every if e[1] == h] for h in range(split, raw_hops, -1)]
    order = sum(batches, [])
    base_of = [sum(len(b) for b in batches[:i]) for i in range(len(batches))]

    def ring_of(sign):
        return core if sign == 1 else 1 - core

    def extract(ring_, h):
        k = 0 if ring_ is None else slot_of(ring_.index, h)
        targets = lax.broadcasted_iota(I32, (block, bins), 0) + block * grp
        v = v_ref[...] if ring_ is None else vbuf[ring_.index, h - 1]
        ext[k] = pick(targets, v, raw_rows(ring_, h))

    def compact(ring_, distances):
        pieces = []
        for d in distances:
            first, count = ring_.tail_rows(d)
            dest = group_at(ring_.sign, d - raw_hops)
            pieces.append(lax.broadcasted_iota(I32, (count, bins), 0) + (block * dest + first))
        targets = jnp.concatenate(pieces, axis=0)
        picked = pick(targets, vbuf[ring_.index, raw_hops - 1], raw_rows(ring_, raw_hops))
        at = 0
        for d in distances:
            _, count = ring_.tail_rows(d)
            dbuf[ring_.index, half - d, pl.ds(0, count)] = picked[at:at + count]
            at += count

    def routed_rows(k, s):
        sign, h = k
        if h <= raw_hops:
            at = 0 if h == 0 else 2 * h - 1 + ring_of(sign)
            return ext[at, pl.ds(s * MOST, MOST)]
        if h < half:
            return cbuf[ring_of(sign), messages.index((h, h)), pl.ds(s * MOST, MOST)]
        for each in rings:
            first, count = each.tail_rows(half)
            if first <= s * MOST < first + count:
                return cbuf[each.index, messages.index((half, half)), pl.ds(s * MOST - first, MOST)]

    per_tile = half
    lanes = per_tile * MOST
    share = mp.shape[1] // m_all

    def pieces_of(batch):
        return [(e, s) for s in range(slots) for e in batches[batch]]

    def tiles_of(batch):
        return -(-len(pieces_of(batch)) // per_tile)

    def fine_matmul(batch):
        pieces = pieces_of(batch)
        for t in range(tiles_of(batch)):
            here = pieces[t * per_tile:(t + 1) * per_tile]
            total = None
            for s in sorted({piece[1] for piece in here}):
                parts = [routed_rows(e, s) if slot == s else jnp.zeros((MOST, width), BF) for e, slot in here]
                parts += [jnp.zeros((MOST, width), BF)] * (per_tile - len(here))
                product = lax.dot_general(mp[s], jnp.concatenate(parts, axis=0), (((1,), (1,)), ((), ())),
                                          preferred_element_type=F32)
                total = product if total is None else total + product
            part[batch, :, t] = total.reshape(m_all, share, lanes)

    def reduce_copy(batch, i):
        to = lax.rem(mem + i, m_all)
        count = tiles_of(batch)
        return remote(part.at[batch, to, pl.ds(0, count)], red.at[batch, i - 1, pl.ds(0, count)],
                      rs.at[batch], rr.at[batch], {"grp": grp, "mem": to})

    def reduce_start(batch):
        @pl.loop(1, m_all)
        def _(i):
            reduce_copy(batch, i).start()

    def all_reduced(batch, sem):
        whole = red.at[batch, :, pl.ds(0, tiles_of(batch))]
        return pltpu.make_async_copy(whole, whole, sem)

    returns = {}

    def reduce_finish(batch):
        all_reduced(batch, rr.at[batch]).wait()
        count = tiles_of(batch)
        total = part[batch, mem, pl.ds(0, count)] + jnp.sum(red[batch, :, pl.ds(0, count)], axis=0)
        lane = lax.broadcasted_iota(I32, (share, lanes), 1)
        pieces = pieces_of(batch)
        for k, entry in enumerate(batches[batch]):
            tile = jnp.zeros((share, lanes), F32)
            for s in range(slots):
                p = pieces.index((entry, s))
                moved = pltpu.roll(total[p // per_tile], (MOST * (s - p % per_tile)) % lanes, 1)
                tile = jnp.where((lane >= MOST * s) & (lane < MOST * (s + 1)), moved, tile)
            at = base_of[batch] + k
            if at == 0:
                ret[at] = tile
            else:
                sums[at] = tile
        for k, (sign, h) in enumerate(batches[batch]):
            at = base_of[batch] + k
            if at > 0:
                copy = remote(sums.at[at], ret.at[at], ts.at[at], tr.at[at],
                              {"grp": lax.rem(grp - sign * h + n, n), "mem": mem})
                copy.start()
                returns[at] = copy

    total_rounds = raw_hops * CHUNKS
    steps = {}

    def at_round(r, action):
        steps.setdefault(r, []).append(action)

    stride = max(1, total_rounds // half)
    for h in range(0, half + 1):
        for ring_ in rings:
            if h > ring_.coarse_hops() or (h == 0 and ring_.index == 1):
                continue
            k = slot_of(ring_.index, h)
            base = stride * h

            def arrive(ring_=ring_, h=h, k=k):
                if h > 0:
                    ring_.coarse[h].wait_recv()
                    if h < ring_.coarse_hops():
                        ring_.send_coarse(h + 1)
                else:
                    own_copy.wait()
                spread_step(k, source_of(ring_, h), 0)

            at_round(base, arrive)
            for phase in (1, 2, 3):
                at_round(base + stride * phase + phase,
                         functools.partial(spread_step, k, source_of(ring_, h), phase))

            def multiply(ring_=ring_, h=h):
                if h == 0:
                    rep_copy.wait()
                coarse_matmul(source_of(ring_, h))

            at_round(base + stride * 3 + 3, multiply)

    at_round(2, functools.partial(extract, None, 0))
    for h in range(1, raw_hops):
        for ring_ in rings:
            at_round((h + 1) * CHUNKS + ring_.index + 1, functools.partial(extract, ring_, h))

    for ring_ in rings:
        ring_.send_coarse(1)
    sizes = []

    def begin_routes():
        sizes.append(route())
        for ring_ in rings:
            ring_.send_idx(1)
        bp_copy.wait()

    at_round(1, begin_routes)
    steps[1] = steps[1][-1:] + steps[1][:-1]
    for r in range(total_rounds):
        for ring_ in rings:
            if r >= CHUNKS:
                if r % CHUNKS == 0:
                    ring_.idx[r // CHUNKS].wait_recv()
                    ring_.send_idx(r // CHUNKS + 1)
                ring_.raw[r - CHUNKS].wait_recv()
            ring_.send_raw(r)
        for action in steps.pop(r, []):
            action()

    for ring_ in rings:
        ring_.idx[raw_hops].wait_recv()
        for r in range(total_rounds - CHUNKS, total_rounds):
            ring_.raw[r].wait_recv()
        compact(ring_, range(half, split, -1))
        ring_.send_compact(0)

    for ring_ in rings:
        at_round(total_rounds + 1, functools.partial(compact, ring_, range(split, raw_hops, -1)))
    at_round(total_rounds + 2, functools.partial(extract, rings[0], raw_hops))
    at_round(total_rounds + 2, functools.partial(extract, rings[1], raw_hops))

    def begin_first():
        mp_copy.wait()
        fine_matmul(0)
        reduce_start(0)

    at_round(total_rounds + 3, begin_first)
    at_round(total_rounds + 9, functools.partial(reduce_finish, 0))

    for k in range(0, len(messages)):
        for ring_ in rings:
            if k > 0:
                ring_.send_compact(k)
        for action in steps.pop(total_rounds + k, []):
            action()
    for r in sorted(steps):
        for action in steps[r]:
            action()

    for batch in range(1, len(batches)):
        for h in sorted({h for _, h in batches[batch]}):
            for ring_ in rings:
                ring_.compact[messages.index((h, h))].wait_recv()
        fine_matmul(batch)
        reduce_start(batch)
    for ring_ in rings:
        ring_.drain()
    for phase in range(3):
        bytes_of(phase, n, xs.at[phase]).wait()
    for batch in range(1, len(batches)):
        reduce_finish(batch)
    for at in returns:
        returns[at].wait_recv()

    gathered = jnp.concatenate([ret[k] for k in range(n)], axis=1)
    high = gathered.astype(BF).astype(F32)
    rest = gathered - high
    middle = rest.astype(BF).astype(F32)
    low = rest - middle
    spare = jnp.zeros((-3 * share % 16, n * lanes), F32)
    lhs = jnp.concatenate([high, middle, low, spare], axis=0).astype(BF)
    q = lax.broadcasted_iota(I32, (lanes, bins), 0)
    targets = []
    for sign, h in order:
        owner = lax.rem(grp + sign * h + n, n)
        targets.append(jnp.where(q < block, q + block * owner, -1))
    targets = jnp.concatenate(targets, axis=0)
    for r in range(2):
        chosen = jnp.where(targets == v_ref[r:r + 1, :], 1.0, 0.0).astype(BF)
        got = jnp.dot(lhs, chosen, preferred_element_type=F32)
        whole = got[0:share] + got[share:2 * share] + got[2 * share:3 * share]
        column = (lax.broadcasted_iota(I32, (share, bins), 0) + mem * share).astype(F32)
        live = column < sizes[0][:, r * bins:(r + 1) * bins]
        fine_ref[r] = jnp.where(live, whole * (width * m_all) ** (-0.5), 0.0)

    for batch in range(len(batches)):
        all_reduced(batch, rs.at[batch]).wait()
    for at in returns:
        returns[at].wait_send()


def local(bin_sketch, rep_sketch, bin_profile, member_profile, bin_routes, owner_slot, cluster_sizes, raw=RAW):
    bins, width = bin_profile.shape
    slots, members, _ = member_profile.shape
    bin_dev, w = bin_sketch.shape
    reps = rep_sketch.shape[0]
    n, m_all = lax.axis_size("grp"), lax.axis_size("mem")
    edge = int(round((m_all // 2) ** 0.5))
    half = n // 2
    share = members // m_all
    cluster_total = owner_slot.shape[0]
    block = slots * MOST
    lanes = half * MOST
    messages = compact_list(half, raw)

    groups = 2 + (half + raw) // 2 - raw
    z_sends = half + raw + raw * CHUNKS + len(messages)
    cfg = {"n": n, "m": m_all, "edge": edge, "raw": raw}
    vmem = pl.BlockSpec(memory_space=pltpu.VMEM)
    hbm = pl.BlockSpec(memory_space=pltpu.HBM)
    dma = pltpu.SemaphoreType.DMA
    coarse, fine = pl.pallas_call(
        functools.partial(screen, cfg),
        out_shape=(
            pltpu.VMEM((n, edge, edge, 2, bin_dev, reps), BF),
            pltpu.VMEM((2, share, bins), F32),
        ),
        in_specs=[hbm, hbm, hbm, hbm, vmem, vmem, vmem],
        out_specs=(vmem, vmem),
        scratch_shapes=[
            pltpu.VMEM((bins, width), BF),
            pltpu.VMEM((8, bins), I32),
            pltpu.VMEM((2, raw * CHUNKS, bins // CHUNKS, width), BF),
            pltpu.VMEM((2, raw, 8, bins), I32),
            pltpu.VMEM((2, len(messages), block, width), BF),
            pltpu.VMEM((2, half - raw, block, width), BF),
            pltpu.VMEM((2 * raw + 1, block, width), BF),
            pltpu.VMEM((n, 2, edge, edge, bin_dev, w), BF),
            pltpu.VMEM((reps, w), BF),
            pltpu.VMEM((slots, members, width), BF),
            pltpu.VMEM((groups, m_all, slots, share, lanes), F32),
            pltpu.VMEM((groups, m_all - 1, slots, share, lanes), F32),
            pltpu.VMEM((n, share, lanes), F32),
            pltpu.VMEM((n, share, lanes), F32),
            dma((2, QUEUE)), dma((2, z_sends)),
            dma((3,)), dma((n, 3)),
            dma((groups,)), dma((groups,)),
            dma((n,)), dma((n,)),
            dma((4,)),
        ],
        compiler_params=pltpu.CompilerParams(
            collective_id=0, has_side_effects=True, vmem_limit_bytes=64749568),
    )(bin_sketch, rep_sketch, bin_profile, member_profile, bin_routes.T, owner_slot[None], cluster_sizes[None])
    return (coarse.reshape(n * m_all * bin_dev, reps), fine.transpose(2, 0, 1))


def solution(mesh):
    return jax.shard_map(
        local,
        mesh=mesh,
        in_specs=(
            P(("grp", "mem"), None),
            P(("grp", "mem"), None),
            P("grp", "mem"),
            P("grp", None, "mem"),
            P("grp", None),
            P(),
            P(),
        ),
        out_specs=(P(None, ("grp", "mem")), P("grp", None, "mem")),
        check_vma=False,
    )
```
